32 devices in a mesh: sec: 4 (over y, core), brick: 8 (over z, x).
Axes of the slice: x: 2, y: 2, z: 4, core: 2. Of those that a mesh axis runs over, the one named last changes fastest.
Arguments:
- tokens: bfloat16 [64, 128, 16, 384], P(('sec', 'brick')), may hold values from -6 to 6
- tissue: int32 [8, 16, 2, 512], P('sec', 'brick'), may hold values from 0 to 1, as said below
- norm1_gain: float32 [384], replicated, may hold values from 0.1 to 1.9
- qkv_weight: bfloat16 [384, 1152], replicated, may hold values from -0.3125 to 0.3125
- position_bias: bfloat16 [12, 512, 512], replicated, may hold values from -4 to 250
- out_weight: bfloat16 [384, 384], replicated, may hold values from -0.3125 to 0.3125
- norm2_gain: float32 [384], replicated, may hold values from 0.1 to 1.9
- up_weight: bfloat16 [384, 1536], replicated, may hold values from -0.3125 to 0.3125
- down_weight: bfloat16 [1536, 384], replicated, may hold values from -0.15625 to 0.15625
Outputs:
- layer_out: bfloat16 [64, 128, 16, 384], P('sec', 'brick')
The draws below stay inside these ranges and needn't reach their ends.
Inputs may be any that keep to these rules, and one draw needn't show every extreme that they name: `tissue`: window (a, b, c) lies on the device of sec index a // 2 and brick index b // 2. Of the 8 windows of one device at most 6 hold any 1, and in every draw some device has exactly 6 such windows; every other window is all 0.
All inputs are finite; a program needn't handle non-finite values.
Results may differ from the reference program's by a relative error of at most 0.003.
Values may be sent and summed in bfloat16 or wider, within the bound.
A program may use at most 128 MiB of HBM per device.

```python
import jax
import jax.numpy as jnp
from jax import lax

D = 384
HEADS = 12
MLP_UNITS = 1536
WIN = 8
SHIFT = 4
WINDOW_TOKENS = 512
BZ = 16
BY = 16
BX = 16
LIVE_MOST = 6
VOL_Z = 64
VOL_Y = 128
VOL_X = 16
N_SEC = 4
N_BRICK = 8


def draw_tissue(key, part):
    count_z = BZ // WIN
    count_y = BY // WIN
    count_x = BX // WIN
    per_device = count_z * count_y * count_x
    devices = N_SEC * N_BRICK
    count_key, busy_key, order_key, token_key, spot_key = jax.random.split(key, 5)
    counts = jax.random.randint(count_key, (devices,), 1, max(LIVE_MOST // 2, 1) + 1)
    busiest = jax.random.randint(busy_key, (), 0, devices)
    counts = jnp.where(jnp.arange(devices) == busiest, LIVE_MOST, counts)

    def shuffled(subkey):
        return jax.random.permutation(subkey, per_device)
    window_rank = jax.vmap(shuffled)(jax.random.split(order_key, devices))
    alive_mask = window_rank < counts[:, None]
    tokens_on = jax.random.randint(token_key, (devices, per_device, WINDOW_TOKENS), 0, 4) < 3
    forced_spot = jax.random.randint(spot_key, (devices, per_device, 1), 0, WINDOW_TOKENS)
    tokens_on = tokens_on | (jnp.arange(WINDOW_TOKENS)[None, None, :] == forced_spot)
    tissue_marks = (alive_mask[:, :, None] & tokens_on).astype(jnp.int32)
    tissue_marks = tissue_marks.reshape(N_SEC, N_BRICK, count_z, count_y, count_x, WINDOW_TOKENS)
    tissue_marks = tissue_marks.transpose(0, 2, 1, 3, 4, 5)
    return tissue_marks.reshape(N_SEC * count_z, N_BRICK * count_y, count_x, WINDOW_TOKENS)


def draw_position_bias(key, part):
    shape = (HEADS, WINDOW_TOKENS, WINDOW_TOKENS)
    base_key = jax.random.fold_in(key, 0)
    return jnp.clip(jax.random.normal(base_key, shape, jnp.float32), -4.0, 4.0).astype(jnp.bfloat16)


def level_of(stream_key, extent, cuts, smallest, high):
    gain = 1.0
    for dim, blocks in cuts:
        draws = jax.random.uniform(jax.random.fold_in(jax.random.fold_in(stream_key, 6), dim), (blocks,), jnp.float32, smallest / len(cuts), high / len(cuts))
        gain = gain * jnp.repeat(jnp.exp(draws), extent[dim] // blocks).reshape((-1,) + (1,) * (len(extent) - 1 - dim))
    return gain


def noise(rng, shape, scale, most, cuts=(), dtype=jnp.bfloat16):
    entries = scale * jax.random.normal(rng, shape, jnp.float32)
    if cuts:
        entries = entries * level_of(rng, shape, cuts, -0.22, 0.18)
    return jnp.clip(entries, -most, most).astype(dtype)


def setup_inputs(seed: int = 0) -> dict:
    key_list = jax.random.split(jax.random.key(seed), 10)
    return {
        "tokens": noise(key_list[0], (VOL_Z, VOL_Y, VOL_X, D), 1.0, 6.0, ((0, 32),)),
        "tissue": draw_tissue(jax.random.fold_in(key_list[9], 71), 0),
        "norm1_gain": jnp.clip(1.0 + 0.18 * jax.random.normal(key_list[2], (D,), jnp.float32), 0.1, 1.9),
        "qkv_weight": noise(key_list[3], (D, 3 * D), D ** -0.5, 0.3125),
        "position_bias": draw_position_bias(jax.random.fold_in(key_list[9], 71), 0),
        "out_weight": noise(key_list[5], (D, D), D ** -0.5, 0.3125),
        "norm2_gain": jnp.clip(1.0 + 0.18 * jax.random.normal(key_list[6], (D,), jnp.float32), 0.1, 1.9),
        "up_weight": noise(key_list[7], (D, MLP_UNITS), D ** -0.5, 0.3125),
        "down_weight": noise(key_list[8], (MLP_UNITS, D), MLP_UNITS ** -0.5, 0.15625),
    }


EPS = 1e-05

def layer_norm(values, gain_row):
    values = values.astype(jnp.float32)
    centered = values - lax.optimization_barrier(jnp.mean(values, axis=-1, keepdims=True))
    variance = lax.optimization_barrier(jnp.mean(centered * centered, axis=-1, keepdims=True))
    return centered * lax.rsqrt(variance + EPS) * gain_row

def cut_windows(volume):
    depth_cells, height, across, features = volume.shape
    count_z, count_y, count_x = (depth_cells // WIN, height // WIN, across // WIN)
    blocks = volume.reshape(count_z, WIN, count_y, WIN, count_x, WIN, features)
    return blocks.transpose(0, 2, 4, 1, 3, 5, 6).reshape(count_z * count_y * count_x, WIN ** 3, features)

def join_windows(windows, depth_cells, height, across):
    features = windows.shape[-1]
    count_z, count_y, count_x = (depth_cells // WIN, height // WIN, across // WIN)
    blocks = windows.reshape(count_z, count_y, count_x, WIN, WIN, WIN, features)
    return blocks.transpose(0, 3, 1, 4, 2, 5, 6).reshape(depth_cells, height, across, features)

def window_block(windows, tissue_rows, labels, norm1_gain, qkv_weight, position_bias, out_weight, norm2_gain, up_weight, down_weight):
    groups, length, model_width = windows.shape
    head_count = position_bias.shape[0]
    head_size = model_width // head_count
    flat_rows = windows.reshape(groups * length, model_width)
    normed = layer_norm(flat_rows, norm1_gain).astype(jnp.bfloat16)
    projected = jnp.dot(normed, qkv_weight, preferred_element_type=jnp.float32).astype(jnp.bfloat16)
    projected = projected.reshape(groups, length, 3, head_count, head_size)
    queries = projected[:, :, 0].astype(jnp.float32)
    keys_all = projected[:, :, 1].astype(jnp.float32)
    values_all = projected[:, :, 2].astype(jnp.float32)
    scores = jnp.einsum('gqhd,gkhd->ghqk', queries, keys_all) * head_size ** (-0.5)
    scores = scores + position_bias.astype(jnp.float32)[None]
    allowed = (tissue_rows[:, None, :] == 1) & (labels[:, :, None] == labels[:, None, :])
    scores = jnp.where(allowed[:, None], scores, -1e+30)
    row_top = lax.optimization_barrier(jnp.max(scores, axis=-1, keepdims=True))
    raised = jnp.exp(scores - row_top)
    attention = (raised / lax.optimization_barrier(jnp.sum(raised, axis=-1, keepdims=True))).astype(jnp.bfloat16)
    mixed = jnp.einsum('ghqk,gkhd->gqhd', attention.astype(jnp.float32), values_all).astype(jnp.bfloat16)
    mixed = mixed.reshape(groups * length, model_width)
    attended = flat_rows.astype(jnp.float32) + jnp.dot(mixed, out_weight, preferred_element_type=jnp.float32)
    normed_two = layer_norm(attended, norm2_gain).astype(jnp.bfloat16)
    feed = jax.nn.gelu(jnp.dot(normed_two, up_weight, preferred_element_type=jnp.float32), approximate=False).astype(jnp.bfloat16)
    result = attended + jnp.dot(feed, down_weight, preferred_element_type=jnp.float32)
    keep_token = tissue_rows.reshape(groups * length, 1) == 1
    result = jnp.where(keep_token, result, flat_rows.astype(jnp.float32)).astype(jnp.bfloat16)
    return result.reshape(groups, length, model_width)

def reference(tokens, tissue, norm1_gain, qkv_weight, position_bias, out_weight, norm2_gain, up_weight, down_weight):
    depth_cells, height, across, model_width = tokens.shape
    rolled = jnp.roll(tokens, (-SHIFT, -SHIFT, -SHIFT), axis=(0, 1, 2))
    windows = cut_windows(rolled)
    count = windows.shape[0]
    depth_index = lax.broadcasted_iota(jnp.int32, (depth_cells, height, across, 1), 0)
    height_index = lax.broadcasted_iota(jnp.int32, (depth_cells, height, across, 1), 1)
    across_index = lax.broadcasted_iota(jnp.int32, (depth_cells, height, across, 1), 2)
    label_grid = 4 * (depth_index >= depth_cells - SHIFT).astype(jnp.int32)
    label_grid = label_grid + 2 * (height_index >= height - SHIFT).astype(jnp.int32)
    label_grid = label_grid + (across_index >= across - SHIFT).astype(jnp.int32)
    labels = cut_windows(label_grid)[:, :, 0]
    tissue_rows = tissue.reshape(count, WIN ** 3)
    batch = 4 if count % 4 == 0 else 1

    def one_group(packed):
        group_windows, group_tissue, group_labels = packed
        return window_block(group_windows, group_tissue, group_labels, norm1_gain, qkv_weight, position_bias, out_weight, norm2_gain, up_weight, down_weight)
    blocks = lax.map(one_group, (windows.reshape(count // batch, batch, WIN ** 3, model_width), tissue_rows.reshape(count // batch, batch, WIN ** 3), labels.reshape(count // batch, batch, WIN ** 3)))
    blocks = blocks.reshape(count, WIN ** 3, model_width)
    volume = join_windows(blocks, depth_cells, height, across)
    return jnp.roll(volume, (SHIFT, SHIFT, SHIFT), axis=(0, 1, 2))
```

```python
import functools

import jax
import jax.numpy as jnp
from jax import lax
from jax.experimental import pallas as pl
from jax.experimental.pallas import tpu as pltpu
from jax.sharding import PartitionSpec as P

WIN = 8
SHIFT = 4
EPS = 1e-05
TOKENS = WIN**3
LANES = 128
MASKED = -1e30
ROWS = 256
UNITS = 512


def layer_norm(values, gain_row):
    centered = values - jnp.mean(values, axis=-1, keepdims=True)
    variance = jnp.mean(centered * centered, axis=-1, keepdims=True)
    return centered * lax.rsqrt(variance + EPS) * gain_row


def gelu(v):
    return 0.5 * v * (1.0 + lax.erf(v * (0.5**0.5)))


def block_kernel(
    facts,
    x_ref,
    tissue_ref,
    gain1_ref,
    qkv_ref,
    bias_ref,
    out_w_ref,
    gain2_ref,
    up_ref,
    down_ref,
    o_ref,
    win,
    qkv,
    mix,
    key_mask,
    label_hot,
    kept,
    *,
    head_size,
):
    a = pl.program_id(0)
    count_a = pl.num_programs(0)
    width = x_ref.shape[-1]
    heads_per_group = LANES // head_size
    groups = width // LANES
    live_any = facts[2 + 2 * a] + facts[3 + 2 * a]

    @pl.when(live_any == 0)
    def _():
        o_ref[...] = x_ref[...]

    @pl.when(live_any > 0)
    def _():
        cells = x_ref[...].astype(jnp.float32).reshape(WIN * WIN, 2 * WIN, width)
        cells = pltpu.roll(cells, 2 * WIN - SHIFT, 1)
        win[0] = cells[:, :WIN].reshape(TOKENS, width)
        win[1] = cells[:, WIN:].reshape(TOKENS, width)

        @pl.loop(0, 2)
        def _(c):
            @pl.when(facts[2 + 2 * a + c] > 0)
            def _():
                z_last = jnp.where(a == count_a - 1, facts[0], 0)
                y_last = facts[1]
                token = lax.broadcasted_iota(jnp.int32, (TOKENS, LANES), 0)
                lane = lax.broadcasted_iota(jnp.int32, (TOKENS, LANES), 1)
                fz = ((token // (WIN * WIN)) >= SHIFT).astype(jnp.int32) * z_last
                fy = (((token // WIN) % WIN) >= SHIFT).astype(jnp.int32) * y_last
                fx = ((token % WIN) >= SHIFT).astype(jnp.int32) * c
                label = 4 * fz + 2 * fy + fx
                here = label == lane
                marks = tissue_ref[0, c].astype(jnp.float32)
                marks = jnp.broadcast_to(marks.reshape(1, TOKENS), (LANES, TOKENS)).T
                kept[...] = marks
                label_hot[...] = jnp.where(here, 1.0, 0.0).astype(jnp.bfloat16)
                key_mask[...] = jnp.where(here & (marks > 0.5), 0.0, MASKED).astype(jnp.bfloat16)

                x = win[c]
                normed = layer_norm(x, gain1_ref[...]).astype(jnp.bfloat16)
                scale = head_size ** (-0.5)
                qkv[:, :width] = (
                    jnp.dot(normed, qkv_ref[:, :width], preferred_element_type=jnp.float32) * scale
                ).astype(jnp.bfloat16)
                for part in (1, 2):
                    cols = slice(part * width, (part + 1) * width)
                    qkv[:, cols] = jnp.dot(
                        normed, qkv_ref[:, cols], preferred_element_type=jnp.float32
                    ).astype(jnp.bfloat16)

                @pl.loop(0, groups)
                def _(g):
                    at = pl.multiple_of(g * LANES, LANES)
                    keys = jnp.concatenate(
                        [qkv[:, pl.ds(pl.multiple_of(width + at, LANES), LANES)], key_mask[...]],
                        axis=1,
                    )
                    values = jnp.concatenate(
                        [
                            qkv[:, pl.ds(pl.multiple_of(2 * width + at, LANES), LANES)],
                            jnp.ones((TOKENS, LANES), jnp.bfloat16),
                        ],
                        axis=1,
                    )
                    lane_head = lax.broadcasted_iota(jnp.int32, (ROWS, LANES), 1) // head_size
                    for r in range(TOKENS // ROWS):
                        rows = slice(r * ROWS, (r + 1) * ROWS)
                        queries = qkv[rows, pl.ds(at, LANES)]
                        hot = label_hot[rows, :]
                        total = None
                        for h in range(heads_per_group):
                            mine = lane_head == h
                            query = jnp.where(mine, queries, jnp.zeros_like(queries))
                            scores = lax.dot_general(
                                jnp.concatenate([query, hot], axis=1),
                                keys,
                                (((1,), (1,)), ((), ())),
                                preferred_element_type=jnp.float32,
                            )
                            scores = scores + bias_ref[g * heads_per_group + h, rows, :].astype(
                                jnp.float32
                            )
                            top = jnp.max(scores, axis=-1, keepdims=True)
                            raised = jnp.exp(scores - top).astype(jnp.bfloat16)
                            got = jnp.dot(raised, values, preferred_element_type=jnp.float32)
                            value, weight = got[:, :LANES], got[:, LANES:]
                            if total is None:
                                total, sums = value, weight
                            else:
                                total = jnp.where(mine, value, total)
                                sums = jnp.where(mine, weight, sums)
                        mix[rows, pl.ds(at, LANES)] = (total / sums).astype(jnp.bfloat16)

                attended = x + jnp.dot(
                    mix[...], out_w_ref[...], preferred_element_type=jnp.float32
                )
                normed2 = layer_norm(attended, gain2_ref[...]).astype(jnp.bfloat16)
                result = attended
                for j in range(up_ref.shape[1] // UNITS):
                    units = slice(j * UNITS, (j + 1) * UNITS)
                    feed = gelu(
                        jnp.dot(normed2, up_ref[:, units], preferred_element_type=jnp.float32)
                    ).astype(jnp.bfloat16)
                    result = result + jnp.dot(
                        feed, down_ref[units, :], preferred_element_type=jnp.float32
                    )
                keep = jnp.concatenate([kept[...]] * groups, axis=1) > 0.5
                win[c] = jnp.where(keep, result, win[c])

        cells = jnp.concatenate(
            [
                win[0].reshape(WIN * WIN, WIN, width),
                win[1].reshape(WIN * WIN, WIN, width),
            ],
            axis=1,
        )
        cells = pltpu.roll(cells, SHIFT, 1)
        o_ref[...] = cells.astype(jnp.bfloat16).reshape(o_ref.shape)


def window_rows(facts, cells, tissue, weights):
    gain1, qkv_w, bias, out_w, gain2, up_w, down_w = weights
    depth_cells, height, across, width = cells.shape
    count_a = depth_cells // WIN
    heads = bias.shape[0]
    hidden = up_w.shape[1]

    def whole(array):
        zeros = (0,) * array.ndim
        return pl.BlockSpec(array.shape, lambda a, f: zeros, pipeline_mode=pl.Buffered(1))

    operands = (gain1, qkv_w, bias, out_w, gain2, up_w, down_w)
    tokens = count_a * 2 * TOKENS
    return pl.pallas_call(
        functools.partial(block_kernel, head_size=width // heads),
        out_shape=jax.ShapeDtypeStruct(cells.shape, cells.dtype),
        grid_spec=pltpu.PrefetchScalarGridSpec(
            num_scalar_prefetch=1,
            grid=(count_a,),
            in_specs=[
                pl.BlockSpec((WIN, WIN, across, width), lambda a, f: (a, 0, 0, 0)),
                pl.BlockSpec((1, 2, 1, TOKENS), lambda a, f: (a, 0, 0, 0)),
            ]
            + [whole(array) for array in operands],
            out_specs=pl.BlockSpec((WIN, WIN, across, width), lambda a, f: (a, 0, 0, 0)),
            scratch_shapes=[
                pltpu.VMEM((2, TOKENS, width), jnp.float32),
                pltpu.VMEM((TOKENS, 3 * width), jnp.bfloat16),
                pltpu.VMEM((TOKENS, width), jnp.bfloat16),
                pltpu.VMEM((TOKENS, LANES), jnp.bfloat16),
                pltpu.VMEM((TOKENS, LANES), jnp.bfloat16),
                pltpu.VMEM((TOKENS, LANES), jnp.float32),
            ],
        ),
        compiler_params=pltpu.CompilerParams(
            dimension_semantics=("arbitrary",), vmem_limit_bytes=48 * 2**20
        ),
        cost_estimate=pl.CostEstimate(
            flops=2 * tokens * width * (4 * width + 2 * hidden + 16 * TOKENS),
            bytes_accessed=2 * cells.size * 2 + 2 * bias.size,
            transcendentals=tokens * TOKENS * heads,
        ),
    )(facts, cells, tissue, *operands)


def passed_along(block, axis, distance):
    devices = range(lax.axis_size(axis))
    route = [((i - distance) % len(devices), i) for i in devices]
    return lax.ppermute(block, axis, route)


def passed_across(block, axes):
    outer, inner = (lax.axis_size(axis) for axis in axes)
    route = [
        (i * inner + j, ((i + 1) % outer) * inner + (j + 1) % inner)
        for i in range(outer)
        for j in range(inner)
    ]
    return lax.ppermute(block, axes, route)


def local(tokens, tissue, gain1, qkv_w, bias, out_w, gain2, up_w, down_w):
    planes, rows, across, width = tokens.shape
    bricks = lax.axis_size("brick")
    brick_y = rows // bricks
    sec_last = (lax.axis_index("sec") == lax.axis_size("sec") - 1).astype(jnp.int32)
    brick_last = (lax.axis_index("brick") == bricks - 1).astype(jnp.int32)
    weights = (gain1.reshape(1, width), qkv_w, bias, out_w, gain2.reshape(1, width), up_w, down_w)
    halves = brick_y // WIN
    cut = jnp.roll(tokens, -SHIFT, axis=1).reshape(planes, bricks, halves, WIN, across, width)
    live = jnp.any(tissue == 1, axis=-1).astype(jnp.int32)

    done = {}
    for b in reversed(range(halves)):
        piece = cut[:, :, b].reshape(planes, bricks * WIN, across, width)
        piece = lax.all_to_all(piece, "brick", split_axis=1, concat_axis=0, tiled=True)
        rim = passed_along(piece[:SHIFT], "sec", -1)
        cells = jnp.concatenate([piece[SHIFT:], rim], axis=0)
        y_last = brick_last if b == halves - 1 else jnp.zeros_like(brick_last)
        facts = jnp.concatenate([jnp.stack([sec_last, y_last]), live[:, b].reshape(-1)])
        out = window_rows(facts, cells, tissue[:, b].reshape(-1, 2, 1, TOKENS), weights)
        done[b] = out

    def put_back(out):
        return jnp.concatenate([passed_along(out[-SHIFT:], "sec", 1), out[:-SHIFT]], axis=0)

    last = done[halves - 1]
    over = last[:, -SHIFT:]
    over_y = passed_along(over[:-SHIFT], "brick", 1)
    over_zy = passed_across(over[-SHIFT:], ("sec", "brick"))
    beside = jnp.concatenate([over_zy, over_y], axis=0)
    kept_last = put_back(last[:, :-SHIFT])
    pieces = [beside] + [put_back(done[b]) for b in range(halves - 1)] + [kept_last]
    return jnp.concatenate(pieces, axis=1)


def solution(mesh):
    placed = (
        P(("sec", "brick"), None, None, None),
        P("sec", "brick", None, None),
        P(),
        P(),
        P(),
        P(),
        P(),
        P(),
        P(),
    )
    return jax.shard_map(
        local, mesh=mesh, in_specs=placed, out_specs=P("sec", "brick", None, None), check_vma=False
    )
```

```python
import functools

import jax
import jax.numpy as jnp
from jax import lax
from jax.experimental import pallas as pl
from jax.experimental.pallas import tpu as pltpu
from jax.sharding import PartitionSpec as P

WIN = 8
SHIFT = 4
EPS = 1e-05
TOKENS = WIN**3
LANES = 128
MASKED = -1e30
ROWS = 256
UNITS = 512


def layer_norm(values, gain_row):
    centered = values - jnp.mean(values, axis=-1, keepdims=True)
    variance = jnp.mean(centered * centered, axis=-1, keepdims=True)
    return centered * lax.rsqrt(variance + EPS) * gain_row


def gelu(v):
    return 0.5 * v * (1.0 + lax.erf(v * (0.5**0.5)))


def block_kernel(
    facts,
    x_ref,
    tissue_ref,
    gain1_ref,
    qkv_ref,
    out_w_ref,
    gain2_ref,
    up_ref,
    down_ref,
    bias_hbm,
    o_ref,
    bias_ref,
    qkv,
    mix,
    key_mask,
    label_hot,
    kept,
    bias_sem,
    *,
    head_size,
):
    a = pl.program_id(0)
    count_a = pl.num_programs(0)
    width = x_ref.shape[-1]
    heads_per_group = LANES // head_size
    groups = width // LANES
    live = facts[3 + a] > 0
    bias_copy = pltpu.make_async_copy(bias_hbm, bias_ref, bias_sem)

    @pl.when(a == 0)
    def _():
        bias_copy.start()

    @pl.when(jnp.logical_not(live))
    def _():
        o_ref[...] = x_ref[...]

    @pl.when(live)
    def _():
        z_last = jnp.where(a == count_a - 1, facts[0], 0)
        token = lax.broadcasted_iota(jnp.int32, (TOKENS, LANES), 0)
        lane = lax.broadcasted_iota(jnp.int32, (TOKENS, LANES), 1)
        fz = ((token // (WIN * WIN)) >= SHIFT).astype(jnp.int32) * z_last
        fy = (((token // WIN) % WIN) >= SHIFT).astype(jnp.int32) * facts[1]
        fx = ((token % WIN) >= SHIFT).astype(jnp.int32) * facts[2]
        here = (4 * fz + 2 * fy + fx) == lane
        marks = tissue_ref[0].astype(jnp.float32)
        marks = jnp.broadcast_to(marks, (LANES, TOKENS)).T
        kept[...] = marks
        label_hot[...] = jnp.where(here, 1.0, 0.0).astype(jnp.bfloat16)
        key_mask[...] = jnp.where(here & (marks > 0.5), 0.0, MASKED).astype(jnp.bfloat16)

        normed = layer_norm(x_ref[0].astype(jnp.float32), gain1_ref[...]).astype(jnp.bfloat16)
        scale = head_size ** (-0.5)
        qkv[:, :width] = (
            jnp.dot(normed, qkv_ref[:, :width], preferred_element_type=jnp.float32) * scale
        ).astype(jnp.bfloat16)
        for part in (1, 2):
            cols = slice(part * width, (part + 1) * width)
            qkv[:, cols] = jnp.dot(
                normed, qkv_ref[:, cols], preferred_element_type=jnp.float32
            ).astype(jnp.bfloat16)

    @pl.when(a == 0)
    def _():
        bias_copy.wait()

    @pl.when(live)
    def _():
        @pl.loop(0, groups)
        def _(g):
            at = pl.multiple_of(g * LANES, LANES)
            keys = jnp.concatenate(
                [qkv[:, pl.ds(pl.multiple_of(width + at, LANES), LANES)], key_mask[...]], axis=1
            )
            values = jnp.concatenate(
                [
                    qkv[:, pl.ds(pl.multiple_of(2 * width + at, LANES), LANES)],
                    jnp.ones((TOKENS, LANES), jnp.bfloat16),
                ],
                axis=1,
            )
            lane_head = lax.broadcasted_iota(jnp.int32, (ROWS, LANES), 1) // head_size
            for r in range(TOKENS // ROWS):
                rows = slice(r * ROWS, (r + 1) * ROWS)
                queries = qkv[rows, pl.ds(at, LANES)]
                hot = label_hot[rows, :]
                total = None
                for h in range(heads_per_group):
                    mine = lane_head == h
                    query = jnp.where(mine, queries, jnp.zeros_like(queries))
                    scores = lax.dot_general(
                        jnp.concatenate([query, hot], axis=1),
                        keys,
                        (((1,), (1,)), ((), ())),
                        preferred_element_type=jnp.float32,
                    )
                    scores = scores + bias_ref[g * heads_per_group + h, rows, :].astype(jnp.float32)
                    top = jnp.max(scores, axis=-1, keepdims=True)
                    raised = jnp.exp(scores - top).astype(jnp.bfloat16)
                    got = jnp.dot(raised, values, preferred_element_type=jnp.float32)
                    value, weight = got[:, :LANES], got[:, LANES:]
                    if total is None:
                        total, sums = value, weight
                    else:
                        total = jnp.where(mine, value, total)
                        sums = jnp.where(mine, weight, sums)
                mix[rows, pl.ds(at, LANES)] = (total / sums).astype(jnp.bfloat16)

        x = x_ref[0].astype(jnp.float32)
        attended = x + jnp.dot(mix[...], out_w_ref[...], preferred_element_type=jnp.float32)
        normed2 = layer_norm(attended, gain2_ref[...]).astype(jnp.bfloat16)
        result = attended
        for j in range(up_ref.shape[1] // UNITS):
            units = slice(j * UNITS, (j + 1) * UNITS)
            feed = gelu(
                jnp.dot(normed2, up_ref[:, units], preferred_element_type=jnp.float32)
            ).astype(jnp.bfloat16)
            result = result + jnp.dot(feed, down_ref[units, :], preferred_element_type=jnp.float32)
        keep = jnp.concatenate([kept[...]] * groups, axis=1) > 0.5
        o_ref[0] = jnp.where(keep, result, x).astype(jnp.bfloat16)


def run_windows(facts, windows, tissue, weights):
    gain1, qkv_w, bias, out_w, gain2, up_w, down_w = weights
    count, tokens, width = windows.shape
    heads = bias.shape[0]
    hidden = up_w.shape[1]

    def whole(array):
        zeros = (0,) * array.ndim
        return pl.BlockSpec(array.shape, lambda a, f: zeros, pipeline_mode=pl.Buffered(1))

    operands = (gain1, qkv_w, out_w, gain2, up_w, down_w)
    return pl.pallas_call(
        functools.partial(block_kernel, head_size=width // heads),
        out_shape=jax.ShapeDtypeStruct(windows.shape, windows.dtype),
        grid_spec=pltpu.PrefetchScalarGridSpec(
            num_scalar_prefetch=1,
            grid=(count,),
            in_specs=[
                pl.BlockSpec((1, tokens, width), lambda a, f: (a, 0, 0)),
                pl.BlockSpec((1, 1, tokens), lambda a, f: (a, 0, 0)),
            ]
            + [whole(array) for array in operands]
            + [pl.BlockSpec(memory_space=pl.ANY)],
            out_specs=pl.BlockSpec((1, tokens, width), lambda a, f: (a, 0, 0)),
            scratch_shapes=[
                pltpu.VMEM(bias.shape, jnp.bfloat16),
                pltpu.VMEM((tokens, 3 * width), jnp.bfloat16),
                pltpu.VMEM((tokens, width), jnp.bfloat16),
                pltpu.VMEM((tokens, LANES), jnp.bfloat16),
                pltpu.VMEM((tokens, LANES), jnp.bfloat16),
                pltpu.VMEM((tokens, LANES), jnp.float32),
                pltpu.SemaphoreType.DMA,
            ],
        ),
        compiler_params=pltpu.CompilerParams(
            dimension_semantics=("arbitrary",), vmem_limit_bytes=32 * 2**20
        ),
        cost_estimate=pl.CostEstimate(
            flops=2 * count * tokens * width * (4 * width + 2 * hidden + 16 * tokens),
            bytes_accessed=4 * windows.size + 2 * bias.size,
            transcendentals=count * tokens * tokens * heads,
        ),
    )(facts, windows, tissue, *operands, bias)


def passed_along(block, axis, distance):
    devices = range(lax.axis_size(axis))
    route = [((i - distance) % len(devices), i) for i in devices]
    return lax.ppermute(block, axis, route)


def passed_across(block, axes):
    outer, inner = (lax.axis_size(axis) for axis in axes)
    route = [
        (i * inner + j, ((i + 1) % outer) * inner + (j + 1) % inner)
        for i in range(outer)
        for j in range(inner)
    ]
    return lax.ppermute(block, axes, route)


def local(tokens, tissue, gain1, qkv_w, bias, out_w, gain2, up_w, down_w):
    planes, rows, across, width = tokens.shape
    bricks = lax.axis_size("brick")
    brick_y = rows // bricks
    sec_last = (lax.axis_index("sec") == lax.axis_size("sec") - 1).astype(jnp.int32)
    brick_last = (lax.axis_index("brick") == bricks - 1).astype(jnp.int32)
    weights = (gain1.reshape(1, width), qkv_w, bias, out_w, gain2.reshape(1, width), up_w, down_w)
    halves, sides = brick_y // WIN, across // WIN
    cut = jnp.roll(tokens, (-SHIFT, -SHIFT), axis=(1, 2))
    cut = cut.reshape(planes, bricks, halves, WIN, sides, WIN, width)
    live = jnp.any(tissue == 1, axis=-1).astype(jnp.int32)

    order = [(b, c) for b in reversed(range(halves)) for c in range(sides)]
    pieces = []
    for b, c in order:
        piece = cut[:, :, b, :, c].reshape(planes, bricks * WIN, WIN, width)
        pieces.append(lax.all_to_all(piece, "brick", split_axis=1, concat_axis=0, tiled=True))

    outs = {}
    for step, (b, c) in enumerate(order):
        piece = pieces[step]
        if step > 0:
            piece, outs[order[step - 1]] = lax.optimization_barrier(
                (piece, outs[order[step - 1]])
            )
        rim = passed_along(piece[:SHIFT], "sec", -1)
        windows = jnp.concatenate([piece[SHIFT:], rim], axis=0).reshape(-1, TOKENS, width)
        y_last = brick_last if b == halves - 1 else jnp.zeros_like(brick_last)
        x_last = jnp.full_like(brick_last, int(c == sides - 1))
        facts = jnp.concatenate([jnp.stack([sec_last, y_last, x_last]), live[:, b, c]])
        outs[b, c] = run_windows(facts, windows, tissue[:, b, c][:, None], weights)

    def strip(b, c):
        return outs[b, c].reshape(-1, WIN, WIN, width)

    def put_back(out):
        return jnp.concatenate([passed_along(out[-SHIFT:], "sec", 1), out[:-SHIFT]], axis=0)

    last = jnp.concatenate([strip(halves - 1, c) for c in range(sides)], axis=2)
    over = last[:, -SHIFT:]
    over_y = passed_along(over[:-SHIFT], "brick", 1)
    over_zy = passed_across(over[-SHIFT:], ("sec", "brick"))
    beside = jnp.concatenate([over_zy, over_y], axis=0)
    volume = [beside]
    for b in range(halves - 1):
        volume.append(jnp.concatenate([put_back(strip(b, c)) for c in range(sides)], axis=2))
    volume.append(put_back(last[:, :-SHIFT]))
    return jnp.roll(jnp.concatenate(volume, axis=1), SHIFT, axis=2)


def solution(mesh):
    placed = (
        P(("sec", "brick"), None, None, None),
        P("sec", "brick", None, None),
        P(),
        P(),
        P(),
        P(),
        P(),
        P(),
        P(),
    )
    return jax.shard_map(
        local, mesh=mesh, in_specs=placed, out_specs=P("sec", "brick", None, None), check_vma=False
    )
```

```python
import functools

import jax
import jax.numpy as jnp
from jax import lax
from jax.experimental import pallas as pl
from jax.experimental.pallas import tpu as pltpu
from jax.sharding import PartitionSpec as P

WIN = 8
SHIFT = 4
EPS = 1e-05
TOKENS = WIN**3
LANES = 128
MASKED = -1e30
ROWS = 256
UNITS = 512


def layer_norm(values, gain_row):
    centered = values - jnp.mean(values, axis=-1, keepdims=True)
    variance = jnp.mean(centered * centered, axis=-1, keepdims=True)
    return centered * lax.rsqrt(variance + EPS) * gain_row


def gelu(v):
    return 0.5 * v * (1.0 + lax.erf(v * (0.5**0.5)))


def block_kernel(
    facts,
    x_ref,
    tissue_ref,
    gain1_ref,
    qkv_ref,
    out_w_ref,
    gain2_ref,
    up_ref,
    down_ref,
    bias_hbm,
    o_ref,
    bias_ref,
    win,
    qkv,
    mix,
    key_mask,
    label_hot,
    kept,
    bias_sem,
    *,
    head_size,
):
    a = pl.program_id(0)
    count_a = pl.num_programs(0)
    width = x_ref.shape[-1]
    heads_per_group = LANES // head_size
    groups = width // LANES
    live_any = facts[2 + 2 * a] + facts[3 + 2 * a]
    bias_copy = pltpu.make_async_copy(bias_hbm, bias_ref, bias_sem)

    @pl.when(a == 0)
    def _():
        bias_copy.start()

    @pl.when(live_any == 0)
    def _():
        o_ref[...] = x_ref[...]

    @pl.when(live_any > 0)
    def _():
        cells = x_ref[...].astype(jnp.float32).reshape(WIN * WIN, 2 * WIN, width)
        cells = pltpu.roll(cells, 2 * WIN - SHIFT, 1)
        win[0] = cells[:, :WIN].reshape(TOKENS, width)
        win[1] = cells[:, WIN:].reshape(TOKENS, width)

    @pl.when(a == 0)
    def _():
        bias_copy.wait()

    @pl.when(live_any > 0)
    def _():
        @pl.loop(0, 2)
        def _(c):
            @pl.when(facts[2 + 2 * a + c] > 0)
            def _():
                z_last = jnp.where(a == count_a - 1, facts[0], 0)
                y_last = facts[1]
                token = lax.broadcasted_iota(jnp.int32, (TOKENS, LANES), 0)
                lane = lax.broadcasted_iota(jnp.int32, (TOKENS, LANES), 1)
                fz = ((token // (WIN * WIN)) >= SHIFT).astype(jnp.int32) * z_last
                fy = (((token // WIN) % WIN) >= SHIFT).astype(jnp.int32) * y_last
                fx = ((token % WIN) >= SHIFT).astype(jnp.int32) * c
                label = 4 * fz + 2 * fy + fx
                here = label == lane
                marks = tissue_ref[0, c].astype(jnp.float32)
                marks = jnp.broadcast_to(marks.reshape(1, TOKENS), (LANES, TOKENS)).T
                kept[...] = marks
                label_hot[...] = jnp.where(here, 1.0, 0.0).astype(jnp.bfloat16)
                key_mask[...] = jnp.where(here & (marks > 0.5), 0.0, MASKED).astype(jnp.bfloat16)

                x = win[c]
                normed = layer_norm(x, gain1_ref[...]).astype(jnp.bfloat16)
                scale = head_size ** (-0.5)
                qkv[:, :width] = (
                    jnp.dot(normed, qkv_ref[:, :width], preferred_element_type=jnp.float32) * scale
                ).astype(jnp.bfloat16)
                for part in (1, 2):
                    cols = slice(part * width, (part + 1) * width)
                    qkv[:, cols] = jnp.dot(
                        normed, qkv_ref[:, cols], preferred_element_type=jnp.float32
                    ).astype(jnp.bfloat16)

                @pl.loop(0, groups)
                def _(g):
                    at = pl.multiple_of(g * LANES, LANES)
                    keys = jnp.concatenate(
                        [qkv[:, pl.ds(pl.multiple_of(width + at, LANES), LANES)], key_mask[...]],
                        axis=1,
                    )
                    values = jnp.concatenate(
                        [
                            qkv[:, pl.ds(pl.multiple_of(2 * width + at, LANES), LANES)],
                            jnp.ones((TOKENS, LANES), jnp.bfloat16),
                        ],
                        axis=1,
                    )
                    lane_head = lax.broadcasted_iota(jnp.int32, (ROWS, LANES), 1) // head_size
                    for r in range(TOKENS // ROWS):
                        rows = slice(r * ROWS, (r + 1) * ROWS)
                        queries = qkv[rows, pl.ds(at, LANES)]
                        hot = label_hot[rows, :]
                        total = None
                        for h in range(heads_per_group):
                            mine = lane_head == h
                            query = jnp.where(mine, queries, jnp.zeros_like(queries))
                            scores = lax.dot_general(
                                jnp.concatenate([query, hot], axis=1),
                                keys,
                                (((1,), (1,)), ((), ())),
                                preferred_element_type=jnp.float32,
                            )
                            scores = scores + bias_ref[g * heads_per_group + h, rows, :].astype(
                                jnp.float32
                            )
                            top = jnp.max(scores, axis=-1, keepdims=True)
                            raised = jnp.exp(scores - top).astype(jnp.bfloat16)
                            got = jnp.dot(raised, values, preferred_element_type=jnp.float32)
                            value, weight = got[:, :LANES], got[:, LANES:]
                            if total is None:
                                total, sums = value, weight
                            else:
                                total = jnp.where(mine, value, total)
                                sums = jnp.where(mine, weight, sums)
                        mix[rows, pl.ds(at, LANES)] = (total / sums).astype(jnp.bfloat16)

                attended = x + jnp.dot(
                    mix[...], out_w_ref[...], preferred_element_type=jnp.float32
                )
                normed2 = layer_norm(attended, gain2_ref[...]).astype(jnp.bfloat16)
                result = attended
                for j in range(up_ref.shape[1] // UNITS):
                    units = slice(j * UNITS, (j + 1) * UNITS)
                    feed = gelu(
                        jnp.dot(normed2, up_ref[:, units], preferred_element_type=jnp.float32)
                    ).astype(jnp.bfloat16)
                    result = result + jnp.dot(
                        feed, down_ref[units, :], preferred_element_type=jnp.float32
                    )
                keep = jnp.concatenate([kept[...]] * groups, axis=1) > 0.5
                win[c] = jnp.where(keep, result, win[c])

        cells = jnp.concatenate(
            [
                win[0].reshape(WIN * WIN, WIN, width),
                win[1].reshape(WIN * WIN, WIN, width),
            ],
            axis=1,
        )
        cells = pltpu.roll(cells, SHIFT, 1)
        o_ref[...] = cells.astype(jnp.bfloat16).reshape(o_ref.shape)


def window_rows(facts, cells, tissue, weights):
    gain1, qkv_w, bias, out_w, gain2, up_w, down_w = weights
    depth_cells, height, across, width = cells.shape
    count_a = depth_cells // WIN
    heads = bias.shape[0]
    hidden = up_w.shape[1]

    def whole(array):
        zeros = (0,) * array.ndim
        return pl.BlockSpec(array.shape, lambda a, f: zeros, pipeline_mode=pl.Buffered(1))

    operands = (gain1, qkv_w, out_w, gain2, up_w, down_w)
    tokens = count_a * 2 * TOKENS
    return pl.pallas_call(
        functools.partial(block_kernel, head_size=width // heads),
        out_shape=jax.ShapeDtypeStruct(cells.shape, cells.dtype),
        grid_spec=pltpu.PrefetchScalarGridSpec(
            num_scalar_prefetch=1,
            grid=(count_a,),
            in_specs=[
                pl.BlockSpec((WIN, WIN, across, width), lambda a, f: (a, 0, 0, 0)),
                pl.BlockSpec((1, 2, 1, TOKENS), lambda a, f: (a, 0, 0, 0)),
            ]
            + [whole(array) for array in operands]
            + [pl.BlockSpec(memory_space=pl.ANY)],
            out_specs=pl.BlockSpec((WIN, WIN, across, width), lambda a, f: (a, 0, 0, 0)),
            scratch_shapes=[
                pltpu.VMEM(bias.shape, jnp.bfloat16),
                pltpu.VMEM((2, TOKENS, width), jnp.float32),
                pltpu.VMEM((TOKENS, 3 * width), jnp.bfloat16),
                pltpu.VMEM((TOKENS, width), jnp.bfloat16),
                pltpu.VMEM((TOKENS, LANES), jnp.bfloat16),
                pltpu.VMEM((TOKENS, LANES), jnp.bfloat16),
                pltpu.VMEM((TOKENS, LANES), jnp.float32),
                pltpu.SemaphoreType.DMA,
            ],
        ),
        compiler_params=pltpu.CompilerParams(
            dimension_semantics=("arbitrary",), vmem_limit_bytes=32 * 2**20
        ),
        cost_estimate=pl.CostEstimate(
            flops=2 * tokens * width * (4 * width + 2 * hidden + 16 * TOKENS),
            bytes_accessed=2 * cells.size * 2 + 2 * bias.size,
            transcendentals=tokens * TOKENS * heads,
        ),
    )(facts, cells, tissue, *operands, bias)


def passed_along(block, axis, distance):
    devices = range(lax.axis_size(axis))
    route = [((i - distance) % len(devices), i) for i in devices]
    return lax.ppermute(block, axis, route)


def passed_across(block, axes):
    outer, inner = (lax.axis_size(axis) for axis in axes)
    route = [
        (i * inner + j, ((i + 1) % outer) * inner + (j + 1) % inner)
        for i in range(outer)
        for j in range(inner)
    ]
    return lax.ppermute(block, axes, route)


def local(tokens, tissue, gain1, qkv_w, bias, out_w, gain2, up_w, down_w):
    planes, rows, across, width = tokens.shape
    bricks = lax.axis_size("brick")
    brick_y = rows // bricks
    sec_last = (lax.axis_index("sec") == lax.axis_size("sec") - 1).astype(jnp.int32)
    brick_last = (lax.axis_index("brick") == bricks - 1).astype(jnp.int32)
    weights = (gain1.reshape(1, width), qkv_w, bias, out_w, gain2.reshape(1, width), up_w, down_w)
    halves = brick_y // WIN
    cut = jnp.roll(tokens, -SHIFT, axis=1).reshape(planes, bricks, halves, WIN, across, width)
    live = jnp.any(tissue == 1, axis=-1).astype(jnp.int32)

    pieces = {}
    for b in reversed(range(halves)):
        piece = cut[:, :, b].swapaxes(0, 1)
        piece = lax.all_to_all(piece, "brick", split_axis=0, concat_axis=0, tiled=True)
        pieces[b] = piece.reshape(bricks * planes, WIN, across, width)

    done = {}
    for b in reversed(range(halves)):
        piece = pieces[b]
        if b + 1 in done:
            piece, done[b + 1] = lax.optimization_barrier((piece, done[b + 1]))
        rim = passed_along(piece[:SHIFT], "sec", -1)
        cells = jnp.concatenate([piece[SHIFT:], rim], axis=0)
        y_last = brick_last if b == halves - 1 else jnp.zeros_like(brick_last)
        facts = jnp.concatenate([jnp.stack([sec_last, y_last]), live[:, b].reshape(-1)])
        out = window_rows(facts, cells, tissue[:, b].reshape(-1, 2, 1, TOKENS), weights)
        done[b] = out

    def put_back(out):
        return jnp.concatenate([passed_along(out[-SHIFT:], "sec", 1), out[:-SHIFT]], axis=0)

    last = done[halves - 1]
    over = last[:, -SHIFT:]
    over_y = passed_along(over[:-SHIFT], "brick", 1)
    over_zy = passed_across(over[-SHIFT:], ("sec", "brick"))
    beside = jnp.concatenate([over_zy, over_y], axis=0)
    kept_last = put_back(last[:, :-SHIFT])
    pieces = [beside] + [put_back(done[b]) for b in range(halves - 1)] + [kept_last]
    return jnp.concatenate(pieces, axis=1)


def solution(mesh):
    placed = (
        P(("sec", "brick"), None, None, None),
        P("sec", "brick", None, None),
        P(),
        P(),
        P(),
        P(),
        P(),
        P(),
        P(),
    )
    return jax.shard_map(
        local, mesh=mesh, in_specs=placed, out_specs=P("sec", "brick", None, None), check_vma=False
    )
```

```python
import functools

import jax
import jax.numpy as jnp
from jax import lax
from jax.experimental import pallas as pl
from jax.experimental.pallas import tpu as pltpu
from jax.sharding import PartitionSpec as P

WIN = 8
SHIFT = 4
EPS = 1e-05
TOKENS = WIN**3
LANES = 128
MASKED = -1e30
ROWS = 256
UNITS = 512


def layer_norm(values, gain_row):
    centered = values - jnp.mean(values, axis=-1, keepdims=True)
    variance = jnp.mean(centered * centered, axis=-1, keepdims=True)
    return centered * lax.rsqrt(variance + EPS) * gain_row


def gelu(v):
    return 0.5 * v * (1.0 + lax.erf(v * (0.5**0.5)))


def block_kernel(
    facts,
    low_ref,
    high_ref,
    rim_ref,
    tissue_ref,
    gain1_ref,
    qkv_ref,
    out_w_ref,
    gain2_ref,
    up_ref,
    down_ref,
    bias_hbm,
    o_ref,
    bias_ref,
    win,
    qkv,
    mix,
    key_mask,
    label_hot,
    kept,
    bias_sem,
    *,
    head_size,
):
    a = pl.program_id(0)
    count_a = pl.num_programs(0)
    width = low_ref.shape[-1]
    heads_per_group = LANES // head_size
    groups = width // LANES
    live_any = facts[2 + 2 * a] + facts[3 + 2 * a]
    bias_copy = pltpu.make_async_copy(bias_hbm, bias_ref, bias_sem)

    @pl.when(a == 0)
    def _():
        bias_copy.start()

    @pl.when(live_any == 0)
    def _():
        o_ref[:SHIFT] = low_ref[...]

        @pl.when(a < count_a - 1)
        def _():
            o_ref[SHIFT:] = high_ref[...]

        @pl.when(a == count_a - 1)
        def _():
            o_ref[SHIFT:] = rim_ref[...]

    @pl.when(live_any > 0)
    def _():
        high = jnp.where(
            a == count_a - 1,
            rim_ref[...].astype(jnp.float32),
            high_ref[...].astype(jnp.float32),
        )
        cells = jnp.concatenate([low_ref[...].astype(jnp.float32), high], axis=0)
        cells = cells.reshape(WIN * WIN, 2 * WIN, width)
        cells = pltpu.roll(cells, 2 * WIN - SHIFT, 1)
        win[0] = cells[:, :WIN].reshape(TOKENS, width)
        win[1] = cells[:, WIN:].reshape(TOKENS, width)

    @pl.loop(0, 2)
    def _(c):
        live = facts[2 + 2 * a + c] > 0

        @pl.when(live)
        def _():
            z_last = jnp.where(a == count_a - 1, facts[0], 0)
            y_last = facts[1]
            token = lax.broadcasted_iota(jnp.int32, (TOKENS, LANES), 0)
            lane = lax.broadcasted_iota(jnp.int32, (TOKENS, LANES), 1)
            fz = ((token // (WIN * WIN)) >= SHIFT).astype(jnp.int32) * z_last
            fy = (((token // WIN) % WIN) >= SHIFT).astype(jnp.int32) * y_last
            fx = ((token % WIN) >= SHIFT).astype(jnp.int32) * c
            label = 4 * fz + 2 * fy + fx
            here = label == lane
            marks = tissue_ref[0, c].astype(jnp.float32)
            marks = jnp.broadcast_to(marks.reshape(1, TOKENS), (LANES, TOKENS)).T
            kept[...] = marks
            label_hot[...] = jnp.where(here, 1.0, 0.0).astype(jnp.bfloat16)
            key_mask[...] = jnp.where(here & (marks > 0.5), 0.0, MASKED).astype(jnp.bfloat16)

            x = win[c]
            normed = layer_norm(x, gain1_ref[...]).astype(jnp.bfloat16)
            scale = head_size ** (-0.5)
            qkv[:, :width] = (
                jnp.dot(normed, qkv_ref[:, :width], preferred_element_type=jnp.float32) * scale
            ).astype(jnp.bfloat16)
            for part in (1, 2):
                cols = slice(part * width, (part + 1) * width)
                qkv[:, cols] = jnp.dot(
                    normed, qkv_ref[:, cols], preferred_element_type=jnp.float32
                ).astype(jnp.bfloat16)

        @pl.when((a == 0) & (c == 0))
        def _():
            bias_copy.wait()

        @pl.when(live)
        def _():
            @pl.loop(0, groups, unroll=True)
            def _(g):
                at = pl.multiple_of(g * LANES, LANES)
                keys = jnp.concatenate(
                    [qkv[:, pl.ds(pl.multiple_of(width + at, LANES), LANES)], key_mask[...]],
                    axis=1,
                )
                values = jnp.concatenate(
                    [
                        qkv[:, pl.ds(pl.multiple_of(2 * width + at, LANES), LANES)],
                        jnp.ones((TOKENS, LANES), jnp.bfloat16),
                    ],
                    axis=1,
                )
                lane_head = lax.broadcasted_iota(jnp.int32, (ROWS, LANES), 1) // head_size
                for r in range(TOKENS // ROWS):
                    rows = slice(r * ROWS, (r + 1) * ROWS)
                    queries = qkv[rows, pl.ds(at, LANES)]
                    hot = label_hot[rows, :]
                    total = None
                    for h in range(heads_per_group):
                        mine = lane_head == h
                        query = jnp.where(mine, queries, jnp.zeros_like(queries))
                        scores = lax.dot_general(
                            jnp.concatenate([query, hot], axis=1),
                            keys,
                            (((1,), (1,)), ((), ())),
                            preferred_element_type=jnp.float32,
                        )
                        scores = scores + bias_ref[g * heads_per_group + h, rows, :].astype(
                            jnp.float32
                        )
                        top = jnp.max(scores, axis=-1, keepdims=True)
                        raised = jnp.exp(scores - top).astype(jnp.bfloat16)
                        got = jnp.dot(raised, values, preferred_element_type=jnp.float32)
                        value, weight = got[:, :LANES], got[:, LANES:]
                        if total is None:
                            total, sums = value, weight
                        else:
                            total = jnp.where(mine, value, total)
                            sums = jnp.where(mine, weight, sums)
                    mix[rows, pl.ds(at, LANES)] = (total / sums).astype(jnp.bfloat16)

            x = win[c]
            attended = x + jnp.dot(
                mix[...], out_w_ref[...], preferred_element_type=jnp.float32
            )
            normed2 = layer_norm(attended, gain2_ref[...]).astype(jnp.bfloat16)
            result = attended
            for j in range(up_ref.shape[1] // UNITS):
                units = slice(j * UNITS, (j + 1) * UNITS)
                feed = gelu(
                    jnp.dot(normed2, up_ref[:, units], preferred_element_type=jnp.float32)
                ).astype(jnp.bfloat16)
                result = result + jnp.dot(
                    feed, down_ref[units, :], preferred_element_type=jnp.float32
                )
            keep = jnp.concatenate([kept[...]] * groups, axis=1) > 0.5
            win[c] = jnp.where(keep, result, x)

    @pl.when(live_any > 0)
    def _():
        cells = jnp.concatenate(
            [
                win[0].reshape(WIN * WIN, WIN, width),
                win[1].reshape(WIN * WIN, WIN, width),
            ],
            axis=1,
        )
        cells = pltpu.roll(cells, SHIFT, 1)
        o_ref[...] = cells.astype(jnp.bfloat16).reshape(o_ref.shape)


def window_rows(facts, cells, rim, tissue, weights):
    gain1, qkv_w, bias, out_w, gain2, up_w, down_w = weights
    depth_cells, height, across, width = cells.shape
    count_a = depth_cells // WIN
    last = depth_cells // SHIFT - 1
    half = (SHIFT, WIN, across, width)
    heads = bias.shape[0]
    hidden = up_w.shape[1]

    def whole(array):
        zeros = (0,) * array.ndim
        return pl.BlockSpec(array.shape, lambda a, f: zeros, pipeline_mode=pl.Buffered(1))

    operands = (gain1, qkv_w, out_w, gain2, up_w, down_w)
    tokens = count_a * 2 * TOKENS
    return pl.pallas_call(
        functools.partial(block_kernel, head_size=width // heads),
        out_shape=jax.ShapeDtypeStruct(cells.shape, cells.dtype),
        grid_spec=pltpu.PrefetchScalarGridSpec(
            num_scalar_prefetch=1,
            grid=(count_a,),
            in_specs=[
                pl.BlockSpec(half, lambda a, f: (1 + 2 * a, 0, 0, 0)),
                pl.BlockSpec(half, lambda a, f: (jnp.minimum(2 + 2 * a, last), 0, 0, 0)),
                pl.BlockSpec(half, lambda a, f: (0, 0, 0, 0)),
                pl.BlockSpec((1, 2, 1, TOKENS), lambda a, f: (a, 0, 0, 0)),
            ]
            + [whole(array) for array in operands]
            + [pl.BlockSpec(memory_space=pltpu.HBM)],
            out_specs=pl.BlockSpec((WIN, WIN, across, width), lambda a, f: (a, 0, 0, 0)),
            scratch_shapes=[
                pltpu.VMEM(bias.shape, jnp.bfloat16),
                pltpu.VMEM((2, TOKENS, width), jnp.float32),
                pltpu.VMEM((TOKENS, 3 * width), jnp.bfloat16),
                pltpu.VMEM((TOKENS, width), jnp.bfloat16),
                pltpu.VMEM((TOKENS, LANES), jnp.bfloat16),
                pltpu.VMEM((TOKENS, LANES), jnp.bfloat16),
                pltpu.VMEM((TOKENS, LANES), jnp.float32),
                pltpu.SemaphoreType.DMA,
            ],
        ),
        compiler_params=pltpu.CompilerParams(
            dimension_semantics=("arbitrary",), vmem_limit_bytes=54 * 2**20
        ),
        cost_estimate=pl.CostEstimate(
            flops=2 * tokens * width * (4 * width + 2 * hidden + 16 * TOKENS),
            bytes_accessed=2 * cells.size * 2 + 2 * bias.size,
            transcendentals=tokens * TOKENS * heads,
        ),
    )(facts, cells, cells, rim, tissue, *operands, bias)


def passed_along(block, axis, distance):
    devices = range(lax.axis_size(axis))
    route = [((i - distance) % len(devices), i) for i in devices]
    return lax.ppermute(block, axis, route)


def passed_across(block, axes):
    outer, inner = (lax.axis_size(axis) for axis in axes)
    route = [
        (i * inner + j, ((i + 1) % outer) * inner + (j + 1) % inner)
        for i in range(outer)
        for j in range(inner)
    ]
    return lax.ppermute(block, axes, route)


def local(tokens, tissue, gain1, qkv_w, bias, out_w, gain2, up_w, down_w):
    planes, rows, across, width = tokens.shape
    bricks = lax.axis_size("brick")
    brick_y = rows // bricks
    sec_last = (lax.axis_index("sec") == lax.axis_size("sec") - 1).astype(jnp.int32)
    brick_last = (lax.axis_index("brick") == bricks - 1).astype(jnp.int32)
    weights = (gain1.reshape(1, width), qkv_w, bias, out_w, gain2.reshape(1, width), up_w, down_w)
    halves = brick_y // WIN
    cut = jnp.roll(tokens, -SHIFT, axis=1).reshape(planes, bricks, halves, WIN, across, width)
    live = jnp.any(tissue == 1, axis=-1).astype(jnp.int32)

    pieces = {}
    for b in reversed(range(halves)):
        piece = cut[:, :, b].swapaxes(0, 1)
        piece = lax.all_to_all(piece, "brick", split_axis=0, concat_axis=0, tiled=True)
        pieces[b] = piece.reshape(bricks * planes, WIN, across, width)

    done = {}
    for b in reversed(range(halves)):
        piece = pieces[b]
        if b + 1 in done:
            piece, done[b + 1] = lax.optimization_barrier((piece, done[b + 1]))
        rim = passed_along(piece[:SHIFT], "sec", -1)
        y_last = brick_last if b == halves - 1 else jnp.zeros_like(brick_last)
        facts = jnp.concatenate([jnp.stack([sec_last, y_last]), live[:, b].reshape(-1)])
        out = window_rows(facts, piece, rim, tissue[:, b].reshape(-1, 2, 1, TOKENS), weights)
        done[b] = out

    def put_back(out):
        return jnp.concatenate([passed_along(out[-SHIFT:], "sec", 1), out[:-SHIFT]], axis=0)

    last = done[halves - 1]
    over = last[:, -SHIFT:]
    over_y = passed_along(over[:-SHIFT], "brick", 1)
    over_zy = passed_across(over[-SHIFT:], ("sec", "brick"))
    beside = jnp.concatenate([over_zy, over_y], axis=0)
    kept_last = put_back(last[:, :-SHIFT])
    pieces = [beside] + [put_back(done[b]) for b in range(halves - 1)] + [kept_last]
    return jnp.concatenate(pieces, axis=1)


def solution(mesh):
    placed = (
        P(("sec", "brick"), None, None, None),
        P("sec", "brick", None, None),
        P(),
        P(),
        P(),
        P(),
        P(),
        P(),
        P(),
    )
    return jax.shard_map(
        local, mesh=mesh, in_specs=placed, out_specs=P("sec", "brick", None, None), check_vma=False
    )
```
